256 devices in a mesh: frame: 64 (over y, x_lo, z), head: 4 (over x_hi, core).
Axes of the slice: x: 4 (x_hi: 2, x_lo: 2; x = x_hi * 2 + x_lo), y: 4, z: 8, core: 2. Of those that a mesh axis runs over, the one named last changes fastest.
Arguments:
- latents: bfloat16 [32768, 5120], P('frame', 'head'), may hold values from -6 to 6
- queries: bfloat16 [32768, 2560], P('frame', 'head'), may hold values from -22 to 22
- keys: bfloat16 [32768, 2560], P('frame', 'head'), may hold values from -6 to 6
- values: bfloat16 [32768, 2560], P('frame', 'head'), may hold values from -6 to 6
- out_weight: bfloat16 [2560, 5120], P('head'), may hold values from -0.5 to 0.5
- gate_table: float32 [4, 5120], P(None, 'head'), may hold values from 0.5 to 2
- levels: int32 [64], P('frame'), may hold values from 0 to 3
- block_mask: int32 [64, 4], P('frame'), may hold values from 0 to 1, as said below
- fresh: bfloat16 [512, 5120], P(None, 'head'), may hold values from -6 to 6
Outputs:
- velocity: bfloat16 [32768, 5120], P('frame', 'head')
- next_latents: bfloat16 [32768, 5120], P('frame', 'head')
The draws below stay inside these ranges and needn't reach their ends.
Inputs may be any that keep to these rules, and one draw needn't show every extreme that they name: block_mask[c, 0] is 1 for every span c.
All inputs are finite; a program needn't handle non-finite values.
Results may differ from the reference program's by a relative error of at most 0.012.
Values may be sent and summed in bfloat16 or wider, within the bound.
No kernel may reach another device: no remote copies, remote signals or barrier semaphores. Data moves between devices by JAX's collectives and lax.ppermute only.
A program may use at most 128 MiB of HBM per device.

```python
import math
import jax
import jax.numpy as jnp
from jax import lax

D = 5120
HEADS = 20
HD = 128
WIN = 4
LEVELS = 4
TOK_DEV = 512
SPANS = 64
TOKENS = 32768
HH = 2560
N_HEAD = 4


def draw_pair(key):
    key_query, key_key = jax.random.split(key, 2)
    query_draw = jnp.clip(jax.random.normal(key_query, (TOKENS, HH), jnp.float32) * 2.0, -12.0, 12.0)
    key_draw = jax.random.normal(key_key, (TOKENS, HH), jnp.float32)
    query_draw = jnp.clip(query_draw, -22.0, 22.0)
    key_draw = jnp.clip(key_draw, -6.0, 6.0)
    return (query_draw, key_draw)


def draw_queries(key, part):
    pair = draw_pair(jax.random.fold_in(key, 17))
    return pair[0].astype(jnp.bfloat16)


def draw_keys(key, part):
    pair = draw_pair(jax.random.fold_in(key, 17))
    return pair[1].astype(jnp.bfloat16)


def draw_block_mask(key, part):
    picks = jax.random.randint(jax.random.fold_in(key, 29), (SPANS, WIN), 0, 10)
    marks = (picks < 7).astype(jnp.int32)
    column = jnp.arange(WIN)[None, :]
    return jnp.where(column == 0, 1, marks).astype(jnp.int32)


def with_ends(entries, rng, smallest, high):
    dims = entries.shape
    index_at = [jax.random.randint(jax.random.fold_in(rng, axis), (), 0, dims[axis]) for axis in range(len(dims))]
    entries = entries.at[tuple(index_at)].set(smallest)
    longest = dims.index(max(dims))
    index_at[longest] = (index_at[longest] + 1) % dims[longest]
    return entries.at[tuple(index_at)].set(high)


def shard_levels(rng, extent, shards, smallest, high):
    level, own = 1.0, jax.random.fold_in(rng, 6)
    for axis_at, parts in shards:
        heights = jnp.exp(jax.random.uniform(jax.random.fold_in(own, axis_at), (parts,), jnp.float32, smallest / len(shards), high / len(shards)))
        level = level * jnp.repeat(heights, extent[axis_at] // parts).reshape([-1 if axis == axis_at else 1 for axis in range(len(extent))])
    return level


def centred(own_key, extent, deviation, reach, cuts=(), kind=jnp.bfloat16):
    entries = deviation * jax.random.normal(own_key, extent, jnp.float32)
    if cuts:
        entries = entries * shard_levels(own_key, extent, cuts, -0.22, 0.18)
    return jnp.clip(entries, -reach, reach).astype(kind)


def setup_inputs(seed: int = 0) -> dict:
    seeds = jax.random.split(jax.random.key(seed), 10)
    latents = centred(seeds[0], (TOKENS, D), 1.0, 6.0, ((0, 64), (1, 4)))
    queries = draw_queries(jax.random.fold_in(seeds[9], 71), 0)
    keys = draw_keys(jax.random.fold_in(seeds[9], 71), 0)
    values = centred(seeds[3], (TOKENS, HH), 1.0, 6.0, ((0, 64), (1, 4)))
    out_weight = centred(seeds[4], (HH, D), HD ** -0.5, 0.5, ((0, 4),))
    gate_table = jnp.clip(0.5 + 1.5 * jax.random.uniform(seeds[5], (LEVELS, D), jnp.float32) ** shard_levels(seeds[5], (LEVELS, D), ((1, 4),), -0.2, 0.2), 0.5, 2.0)
    levels = with_ends(jax.random.randint(seeds[6], (SPANS,), 0, LEVELS), jax.random.fold_in(seeds[6], 1), 0, LEVELS - 1).astype(jnp.int32)
    block_mask = draw_block_mask(jax.random.fold_in(seeds[9], 71), 0)
    fresh = centred(seeds[8], (TOK_DEV, D), 1.0, 6.0, ((1, 4),))
    return dict(latents=latents, queries=queries, keys=keys, values=values, out_weight=out_weight, gate_table=gate_table, levels=levels, block_mask=block_mask, fresh=fresh)


flow_shift = 5.0

def noise_level(point):
    return flow_shift * point / (1.0 + (flow_shift - 1.0) * point)

def reference(latents, queries, keys, values, out_weight, gate_table, levels, block_mask, fresh):
    group = HH // N_HEAD
    scale = 1.0 / math.sqrt(HD)
    padding = jnp.zeros(((WIN - 1) * TOK_DEV, HH), keys.dtype)
    key_padded = jnp.concatenate([padding, keys], 0)
    value_padded = jnp.concatenate([padding, values], 0)

    def one_span(span):
        start = (span * TOK_DEV).astype(jnp.int32)
        query_rows = lax.dynamic_slice_in_dim(queries, start, TOK_DEV, 0).astype(jnp.float32).reshape(TOK_DEV, HEADS, HD)
        key_rows = lax.dynamic_slice_in_dim(key_padded, start, WIN * TOK_DEV, 0).reshape(WIN, TOK_DEV, HEADS, HD)
        key_rows = jnp.flip(key_rows, 0).astype(jnp.float32)
        value_rows = lax.dynamic_slice_in_dim(value_padded, start, WIN * TOK_DEV, 0).reshape(WIN, TOK_DEV, HEADS, HD)
        value_rows = jnp.flip(value_rows, 0).astype(jnp.float32)
        distances = jnp.arange(WIN, dtype=jnp.int32)
        allowed = (block_mask[span] == 1) & (span - distances >= 0)
        scores = jnp.einsum('qhd,bkhd->hqbk', query_rows, key_rows) * scale
        scores = jnp.where(allowed[None, None, :, None], scores, -jnp.inf)
        top = lax.optimization_barrier(jnp.max(scores, axis=(2, 3), keepdims=True))
        expd = jnp.exp(scores - top)
        weights = (expd / lax.optimization_barrier(jnp.sum(expd, axis=(2, 3), keepdims=True))).astype(jnp.bfloat16)
        attended = jnp.einsum('hqbk,bkhd->qhd', weights.astype(jnp.float32), value_rows)
        attended = attended.reshape(TOK_DEV, HH).astype(jnp.bfloat16)
        total = jnp.zeros((TOK_DEV, D), jnp.float32)
        for index in range(N_HEAD):
            part = jnp.dot(attended[:, index * group:(index + 1) * group], out_weight[index * group:(index + 1) * group], preferred_element_type=jnp.float32)
            rounded = lax.optimization_barrier(part.astype(jnp.bfloat16))
            total = total + rounded.astype(jnp.float32)
        return total
    projected = lax.map(one_span, jnp.arange(SPANS, dtype=jnp.int32))
    level_float = levels.astype(jnp.float32)
    delta = noise_level(level_float / LEVELS) - noise_level((level_float + 1.0) / LEVELS)
    gate = gate_table[levels]
    gated = gate[:, None, :] * projected
    velocity = gated.astype(jnp.bfloat16).reshape(TOKENS, D)
    updated = latents.reshape(SPANS, TOK_DEV, D).astype(jnp.float32) + delta[:, None, None] * gated
    moved = updated[1:].reshape((SPANS - 1) * TOK_DEV, D).astype(jnp.bfloat16)
    next_latents = jnp.concatenate([moved, fresh], 0)
    return (velocity, next_latents)
```

```python
import math

import jax
import jax.numpy as jnp
import numpy as np
from jax import lax
from jax.experimental import pallas as pl
from jax.experimental.pallas import tpu as pltpu
from jax.sharding import PartitionSpec as P

HD = 128
LEVELS = 4
flow_shift = 5.0
C = math.log2(math.e) / math.sqrt(HD)
F32 = jnp.float32
BF16 = jnp.bfloat16
NY, NXL, NZ = 4, 2, 8
SIBLING = [(0, 1), (1, 0), (2, 3), (3, 2)]
PARTNER = [(0, 2), (2, 0), (1, 3), (3, 1)]


def noise_level(point):
    return flow_shift * point / (1.0 + (flow_shift - 1.0) * point)


def ring(value, by):
    n = lax.axis_size("frame")
    return lax.ppermute(value, "frame", [(i, (i + by) % n) for i in range(n)])


def swap(value, pairs):
    return lax.ppermute(value, "head", pairs)


NT = (((1,), (1,)), ((), ()))
ON_CHIP = pl.BlockSpec(memory_space=pltpu.VMEM)
SCALARS = pl.BlockSpec(memory_space=pltpu.SMEM)
CHUNK = 256


def attend_first(allow, q_ref, k0, v0, k1, v1, k2, v2, k3, acc_ref, p_ref):
    rows, width = q_ref.shape
    on = [jnp.where(allow[i] == 1, 1.0, 0.0) for i in range(4)]
    for h in range(width // HD):
        hs = pl.ds(h * HD, HD)
        for c in range(rows // CHUNK):
            cs = pl.ds(c * CHUNK, CHUNK)
            q = q_ref[cs, hs]
            s = [lax.dot_general(q, k[:, hs], NT, preferred_element_type=F32) for k in (k0, k1, k2, k3)]
            m = jnp.max(s[0], axis=1, keepdims=True)
            for i in range(1, 4):
                m = jnp.where(allow[i] == 1, jnp.maximum(m, jnp.max(s[i], axis=1, keepdims=True)), m)
            p = [jnp.exp2((s[0] - m) * C)] + [jnp.exp2((s[i] - m) * (C * on[i])) for i in range(1, 4)]
            total = jnp.sum(p[0], axis=1, keepdims=True)
            for i in range(1, 4):
                total += on[i] * jnp.sum(p[i], axis=1, keepdims=True)
            inverse = 1.0 / total
            acc = jnp.dot(p[0].astype(BF16), v0[:, hs], preferred_element_type=F32)
            for i, v in ((1, v1), (2, v2)):
                acc += on[i] * jnp.dot(p[i].astype(BF16), v[:, hs], preferred_element_type=F32)
            acc_ref[cs, hs] = acc * inverse
            p_ref[h, cs, :] = (p[3] * (inverse * on[3])).astype(BF16)


def attend_last(acc_ref, p_ref, v3, o_ref):
    for h in range(v3.shape[1] // HD):
        hs = pl.ds(h * HD, HD)
        o_ref[:, hs] = (acc_ref[:, hs] + jnp.dot(p_ref[h], v3[:, hs], preferred_element_type=F32)).astype(BF16)


def kernel_call(body, ints, args, outs, name, flops, exps=0, space=24):
    moved = sum(a.size * a.dtype.itemsize for a in (*args, *outs))
    return pl.pallas_call(
        body,
        in_specs=[SCALARS] * len(ints) + [ON_CHIP] * len(args),
        out_specs=[ON_CHIP] * len(outs),
        out_shape=outs,
        compiler_params=pltpu.CompilerParams(vmem_limit_bytes=space * 2**20),
        cost_estimate=pl.CostEstimate(flops=flops, transcendentals=exps, bytes_accessed=moved),
        name=name,
    )(*ints, *args)


def project_near(a0, a1, w0, w1, t):
    t[...] = jnp.dot(a0[...], w0[...], preferred_element_type=F32)
    t[...] += jnp.dot(a1[...], w1[...], preferred_element_type=F32)


def project_far(ints, t, a2, a3, w2, w3, gate, columns):
    k = a2.shape[1]
    swapped = ints[1] == 1
    x2 = jnp.where(swapped, a3[...], a2[...])
    x3 = jnp.where(swapped, a2[...], a3[...])
    total = t[:, columns] + jnp.dot(x2, w2[:, columns], preferred_element_type=F32)
    total += jnp.dot(x3, w3[:, columns], preferred_element_type=F32)
    return gate[pl.ds(ints[0], 1), columns] * total


def project_velocity(ints, t, a2, a3, w2, w3, gate, out):
    for j in range(out.shape[1] // CHUNK):
        columns = pl.ds(j * CHUNK, CHUNK)
        out[:, columns] = project_far(ints, t, a2, a3, w2, w3, gate, columns).astype(BF16)


def project_next(ints, delta, t, a2, a3, w2, w3, gate, lat_a, lat_b, fresh, out):
    half = lat_a.shape[0]
    for j in range(out.shape[1] // CHUNK):
        columns = pl.ds(j * CHUNK, CHUNK)
        update = delta[0] * project_far(ints, t, a2, a3, w2, w3, gate, columns)
        for i, lat in enumerate((lat_a, lat_b)):
            rows = pl.ds(i * half, half)
            new = (lat[:, columns].astype(F32) + update[i * half : (i + 1) * half]).astype(BF16)
            out[rows, columns] = jnp.where(ints[2] == 1, fresh[rows, columns], new)


def both(pairs_of):
    pairs = []
    for place in np.ndindex(NY, NXL, NZ, 2, 2):
        (y, x_lo, z, x_hi, core), (y2, x_lo2, z2, x_hi2, core2) = place, pairs_of(*place)
        number = lambda y, x_lo, z, x_hi, core: ((y * NXL + x_lo) * NZ + z) * 4 + x_hi * 2 + core
        pairs.append((number(*place), number(y2, x_lo2, z2, x_hi2, core2)))
    return pairs


def across(value):
    pairs = both(lambda y, x_lo, z, x_hi, core: (y, 1 - x_lo, z, 1 - x_hi, core ^ (y % 2)))
    return lax.ppermute(value, ("frame", "head"), pairs)


def shards(latents, queries, keys, values, out_weight, gate_table, levels, block_mask, fresh):
    frame = lax.axis_index("frame")
    head = lax.axis_index("head")
    spans = lax.axis_size("frame")
    window = block_mask.shape[1]
    rows, width = latents.shape
    rows_w = out_weight.shape[0]
    heads = queries.shape[1] // HD
    barrier = lax.optimization_barrier

    odd = (frame // (NXL * NZ)) % 2
    core = head % 2
    other = (1 - head // 2) * 2 + (core ^ odd)
    columns_of = lambda weight, at: lax.dynamic_slice(weight, (0, at * width), (rows_w, width))

    k_r1 = ring(keys, 1)
    q_next = ring(queries, -1)
    v_r1 = ring(values, 1)
    k_l1 = ring(keys, -1)
    w_far = across(columns_of(out_weight, other))
    meta = jnp.concatenate([block_mask[0], levels])
    k_r1, v_r1, q_next, k_l1, values_, lat_a, lat_b, meta = barrier(
        (k_r1, v_r1, q_next, k_l1, values, latents[: rows // 2], latents[rows // 2 :], meta)
    )

    k_r2 = ring(k_r1, 1)
    v_l1 = ring(values_, -1)
    v_r2 = ring(v_r1, 1)
    lat_a = ring(lat_a, -1)
    meta_next = ring(meta, -1)
    w_far2 = lax.ppermute(
        w_far, "frame", [(i, (((i // 16) ^ 1) * 16) + i % 16) for i in range(NY * NXL * NZ)]
    )

    span = lax.rem(frame + 1, spans)
    distances = jnp.arange(window, dtype=jnp.int32)
    allow = ((meta_next[:window] == 1) & (span - distances >= 0)).astype(jnp.int32)
    work = heads * rows * rows
    half = jax.ShapeDtypeStruct((rows, heads * HD), F32)
    acc, p3 = kernel_call(
        attend_first,
        (allow,),
        (q_next, k_l1, v_l1, keys, values, k_r1, v_r1, k_r2),
        (half, jax.ShapeDtypeStruct((heads, rows, rows), BF16)),
        "attend_first",
        14 * work * HD,
        4 * work,
    )
    v_r2, lat_a, lat_b, out_weight_ = barrier((v_r2, lat_a, lat_b, out_weight))
    (attended,) = kernel_call(
        attend_last,
        (),
        (acc, p3, v_r2),
        (jax.ShapeDtypeStruct((rows, heads * HD), BF16),),
        "attend_last",
        2 * work * HD,
    )

    mine = ring(attended, 1)
    partner1 = swap(attended, PARTNER)
    sibling1 = swap(attended, SIBLING)
    lat_b = ring(lat_b, -1)
    w_own = columns_of(out_weight_, head)
    w_sib = swap(columns_of(out_weight_, head ^ 1), SIBLING)
    near = jax.ShapeDtypeStruct((rows, width), F32)
    flops = 4 * rows * width * heads * HD
    (t1,) = kernel_call(project_near, (), (attended, sibling1, w_own, w_sib), (near,), "near_next", flops)
    partner1, mine, sibling1, w_sib = barrier((partner1, mine, sibling1, w_sib))
    partner2 = swap(mine, PARTNER)
    other1 = swap(partner1, SIBLING)
    sibling2 = swap(mine, SIBLING)

    def scalars(level):
        at = level.astype(F32)
        delta = noise_level(at / LEVELS) - noise_level((at + 1.0) / LEVELS)
        is_last = (frame == spans - 1).astype(jnp.int32)
        return jnp.stack([level, odd, is_last]), delta[None]

    out = jax.ShapeDtypeStruct((rows, width), BF16)
    ints, delta = scalars(meta_next[window])
    (next_latents,) = kernel_call(
        project_next,
        (ints, delta),
        (t1, partner1, other1, w_far, w_far2, gate_table, lat_a, lat_b, fresh),
        (out,),
        "project_next",
        flops,
    )
    (t2,) = kernel_call(project_near, (), (mine, sibling2, w_own, w_sib), (near,), "near_velocity", flops)
    partner2, next_latents, t2 = barrier((partner2, next_latents, t2))
    ints, _ = scalars(levels[0])
    (velocity,) = kernel_call(
        project_velocity,
        (ints,),
        (t2, partner2, swap(partner2, SIBLING), w_far, w_far2, gate_table),
        (out,),
        "project_velocity",
        flops,
    )
    return velocity, next_latents


def solution(mesh):
    in_specs = (
        P("frame", "head"),
        P("frame", "head"),
        P("frame", "head"),
        P("frame", "head"),
        P("head", None),
        P(None, "head"),
        P("frame"),
        P("frame", None),
        P(None, "head"),
    )
    out_specs = (P("frame", "head"), P("frame", "head"))
    return jax.shard_map(shards, mesh=mesh, in_specs=in_specs, out_specs=out_specs, check_vma=False)
```

```python
import math

import jax
import jax.numpy as jnp
import numpy as np
from jax import lax
from jax.experimental import pallas as pl
from jax.experimental.pallas import tpu as pltpu
from jax.sharding import PartitionSpec as P

HD = 128
LEVELS = 4
flow_shift = 5.0
C = math.log2(math.e) / math.sqrt(HD)
F32 = jnp.float32
BF16 = jnp.bfloat16
NY, NXL, NZ = 4, 2, 8
SIBLING = [(0, 1), (1, 0), (2, 3), (3, 2)]
PARTNER = [(0, 2), (2, 0), (1, 3), (3, 1)]


def noise_level(point):
    return flow_shift * point / (1.0 + (flow_shift - 1.0) * point)


def ring(value, by):
    n = lax.axis_size("frame")
    return lax.ppermute(value, "frame", [(i, (i + by) % n) for i in range(n)])


def swap(value, pairs):
    return lax.ppermute(value, "head", pairs)


NT = (((1,), (1,)), ((), ()))
ON_CHIP = pl.BlockSpec(memory_space=pltpu.VMEM)
SCALARS = pl.BlockSpec(memory_space=pltpu.SMEM)
CHUNK = 256
META = 16


def attend_own(meta, q_ref, k, v, o_ref):
    rows, width = q_ref.shape
    for c in range(rows // CHUNK):
        cs = pl.ds(c * CHUNK, CHUNK)
        lane = lax.broadcasted_iota(jnp.int32, (CHUNK, HD), 1)
        side = jnp.zeros((CHUNK, HD), F32)
        for i in range(meta.shape[0]):
            side = jnp.where(lane == META + i, meta[i].astype(F32), side)
        for h in range(width // HD):
            hs = pl.ds(h * HD, HD)
            s = lax.dot_general(q_ref[cs, hs], k[:, hs], NT, preferred_element_type=F32)
            m = jnp.max(s, axis=1, keepdims=True)
            p = jnp.exp2((s - m) * C)
            total = jnp.sum(p, axis=1, keepdims=True)
            o = jnp.dot(p.astype(BF16), v[:, hs], preferred_element_type=F32)
            o_ref[cs, hs] = (o * (1.0 / total)).astype(BF16)
            rest = m * C + jnp.log2(total)
            for i in range(3):
                part = rest.astype(BF16).astype(F32)
                side = jnp.where(lane == 3 * h + i, part, side)
                rest = rest - part
        o_ref[cs, pl.ds(width, HD)] = side.astype(BF16)


def attend_first(allow, q_ref, own, k1, v1, k2, v2, k3, acc_ref, p_ref):
    rows, width = k1.shape
    on = [jnp.where(allow[i] == 1, 1.0, 0.0) for i in range(4)]
    lane = lax.broadcasted_iota(jnp.int32, (CHUNK, HD), 1)
    for h in range(width // HD):
        hs = pl.ds(h * HD, HD)
        for c in range(rows // CHUNK):
            cs = pl.ds(c * CHUNK, CHUNK)
            q = q_ref[cs, hs]
            side = own[cs, pl.ds(width, HD)].astype(F32)
            top = jnp.sum(jnp.where(lane // 3 == h, side, 0.0), axis=1, keepdims=True)
            s = [lax.dot_general(q, k[:, hs], NT, preferred_element_type=F32) for k in (k1, k2, k3)]
            m = top
            for i in range(3):
                m = jnp.where(allow[i + 1] == 1, jnp.maximum(m, jnp.max(s[i], axis=1, keepdims=True) * C), m)
            p = [jnp.exp2((s[i] * C - m) * on[i + 1]) for i in range(3)]
            first = jnp.exp2(top - m)
            total = first
            for i in range(3):
                total += on[i + 1] * jnp.sum(p[i], axis=1, keepdims=True)
            inverse = 1.0 / total
            acc = first * own[cs, hs].astype(F32)
            for i, v in ((0, v1), (1, v2)):
                acc += on[i + 1] * jnp.dot(p[i].astype(BF16), v[:, hs], preferred_element_type=F32)
            acc_ref[cs, hs] = acc * inverse
            p_ref[h, cs, :] = (p[2] * (inverse * on[3])).astype(BF16)


def attend_last(acc_ref, p_ref, v3, o_ref):
    for h in range(v3.shape[1] // HD):
        hs = pl.ds(h * HD, HD)
        o_ref[:, hs] = (acc_ref[:, hs] + jnp.dot(p_ref[h], v3[:, hs], preferred_element_type=F32)).astype(BF16)


def kernel_call(body, ints, args, outs, name, flops, exps=0, space=44):
    moved = sum(a.size * a.dtype.itemsize for a in (*args, *outs))
    return pl.pallas_call(
        body,
        in_specs=[SCALARS] * len(ints) + [ON_CHIP] * len(args),
        out_specs=[ON_CHIP] * len(outs),
        out_shape=outs,
        compiler_params=pltpu.CompilerParams(vmem_limit_bytes=space * 2**20),
        cost_estimate=pl.CostEstimate(flops=1, transcendentals=0, bytes_accessed=1),
        name=name,
    )(*ints, *args)


def project_near(a0, a1, w0, w1, t):
    t[...] = jnp.dot(a0[...], w0[...], preferred_element_type=F32)
    t[...] += jnp.dot(a1[...], w1[...], preferred_element_type=F32)


def project_far(ints, t, a2, a3, w2, w3, gate, columns):
    k = a2.shape[1]
    swapped = ints[1] == 1
    x2 = jnp.where(swapped, a3[...], a2[...])
    x3 = jnp.where(swapped, a2[...], a3[...])
    total = t[:, columns] + jnp.dot(x2, w2[:, columns], preferred_element_type=F32)
    total += jnp.dot(x3, w3[:, columns], preferred_element_type=F32)
    return gate[pl.ds(ints[0], 1), columns] * total


def project_velocity(ints, t, a2, a3, w2, w3, gate, out):
    for j in range(out.shape[1] // CHUNK):
        columns = pl.ds(j * CHUNK, CHUNK)
        out[:, columns] = project_far(ints, t, a2, a3, w2, w3, gate, columns).astype(BF16)


def project_next(ints, delta, t, a2, a3, w2, w3, gate, lat_a, lat_b, fresh, out):
    half = lat_a.shape[0]
    for j in range(out.shape[1] // CHUNK):
        columns = pl.ds(j * CHUNK, CHUNK)
        update = delta[0] * project_far(ints, t, a2, a3, w2, w3, gate, columns)
        for i, lat in enumerate((lat_a, lat_b)):
            rows = pl.ds(i * half, half)
            new = (lat[:, columns].astype(F32) + update[i * half : (i + 1) * half]).astype(BF16)
            out[rows, columns] = jnp.where(ints[2] == 1, fresh[rows, columns], new)


def both(pairs_of):
    pairs = []
    for place in np.ndindex(NY, NXL, NZ, 2, 2):
        (y, x_lo, z, x_hi, core), (y2, x_lo2, z2, x_hi2, core2) = place, pairs_of(*place)
        number = lambda y, x_lo, z, x_hi, core: ((y * NXL + x_lo) * NZ + z) * 4 + x_hi * 2 + core
        pairs.append((number(*place), number(y2, x_lo2, z2, x_hi2, core2)))
    return pairs


def across(value):
    pairs = both(lambda y, x_lo, z, x_hi, core: (y, 1 - x_lo, z, 1 - x_hi, core ^ (y % 2)))
    return lax.ppermute(value, ("frame", "head"), pairs)


def shards(latents, queries, keys, values, out_weight, gate_table, levels, block_mask, fresh):
    frame = lax.axis_index("frame")
    head = lax.axis_index("head")
    spans = lax.axis_size("frame")
    window = block_mask.shape[1]
    rows, width = latents.shape
    rows_w = out_weight.shape[0]
    heads = queries.shape[1] // HD
    barrier = lax.optimization_barrier

    odd = (frame // (NXL * NZ)) % 2
    core = head % 2
    other = (1 - head // 2) * 2 + (core ^ odd)
    columns_of = lambda weight, at: lax.dynamic_slice(weight, (0, at * width), (rows_w, width))

    work = heads * rows * rows
    k_r1 = ring(keys, 1)
    v_r1 = ring(values, 1)
    q_next = ring(queries, -1)
    lat_a = ring(latents[: rows // 2], -1)
    w_far = across(columns_of(out_weight, other))
    (own,) = kernel_call(
        attend_own,
        (jnp.concatenate([block_mask[0], levels]),),
        (queries, keys, values),
        (jax.ShapeDtypeStruct((rows, heads * HD + HD), BF16),),
        "attend_own",
        4 * work * HD,
        work,
    )
    k_r1, v_r1, q_next, lat_a, own = barrier((k_r1, v_r1, q_next, lat_a, own))

    k_r2 = ring(k_r1, 1)
    v_r2 = ring(v_r1, 1)
    own = ring(own, -1)
    own, w_far, lat_b, out_weight_ = barrier((own, w_far, latents[rows // 2 :], out_weight))
    lat_b = ring(lat_b, -1)
    w_far2 = lax.ppermute(
        w_far, "frame", [(i, (((i // 16) ^ 1) * 16) + i % 16) for i in range(NY * NXL * NZ)]
    )
    at = heads * HD + META
    meta_next = own[0, at : at + window + 1].astype(jnp.int32)
    w_own = columns_of(out_weight_, head)
    w_sib = columns_of(out_weight_, head ^ 1)

    span = lax.rem(frame + 1, spans)
    distances = jnp.arange(window, dtype=jnp.int32)
    allow = ((meta_next[:window] == 1) & (span - distances >= 0)).astype(jnp.int32)
    half = jax.ShapeDtypeStruct((rows, heads * HD), F32)
    acc, p3 = kernel_call(
        attend_first,
        (allow,),
        (q_next, own, keys, values, k_r1, v_r1, k_r2),
        (half, jax.ShapeDtypeStruct((heads, rows, rows), BF16)),
        "attend_first",
        10 * work * HD,
        3 * work,
    )
    v_r2, lat_b = barrier((v_r2, lat_b))
    (attended,) = kernel_call(
        attend_last,
        (),
        (acc, p3, v_r2),
        (jax.ShapeDtypeStruct((rows, heads * HD), BF16),),
        "attend_last",
        2 * work * HD,
    )

    attended, w_own, w_sib = barrier((attended, w_own, w_sib))
    mine = ring(attended, 1)
    partner1 = swap(attended, PARTNER)
    sibling1 = swap(attended, SIBLING)
    w_sib = swap(w_sib, SIBLING)
    near = jax.ShapeDtypeStruct((rows, width), F32)
    flops = 4 * rows * width * heads * HD
    (t1,) = kernel_call(project_near, (), (attended, sibling1, w_own, w_sib), (near,), "near_next", flops, space=24)
    partner1, mine, t1 = barrier((partner1, mine, t1))
    partner2 = swap(mine, PARTNER)
    other1 = swap(partner1, SIBLING)
    sibling2 = swap(mine, SIBLING)

    def scalars(level):
        at = level.astype(F32)
        delta = noise_level(at / LEVELS) - noise_level((at + 1.0) / LEVELS)
        is_last = (frame == spans - 1).astype(jnp.int32)
        return jnp.stack([level, odd, is_last]), delta[None]

    out = jax.ShapeDtypeStruct((rows, width), BF16)
    ints, delta = scalars(meta_next[window])
    (next_latents,) = kernel_call(
        project_next,
        (ints, delta),
        (t1, partner1, other1, w_far, w_far2, gate_table, lat_a, lat_b, fresh),
        (out,),
        "project_next",
        flops,
        space=24,
    )
    (t2,) = kernel_call(project_near, (), (mine, sibling2, w_own, w_sib), (near,), "near_velocity", flops, space=24)
    partner2, t2 = barrier((partner2, t2))
    ints, _ = scalars(levels[0])
    (velocity,) = kernel_call(
        project_velocity,
        (ints,),
        (t2, partner2, swap(partner2, SIBLING), w_far, w_far2, gate_table),
        (out,),
        "project_velocity",
        flops,
        space=24,
    )
    return velocity, next_latents


def solution(mesh):
    in_specs = (
        P("frame", "head"),
        P("frame", "head"),
        P("frame", "head"),
        P("frame", "head"),
        P("head", None),
        P(None, "head"),
        P("frame"),
        P("frame", None),
        P(None, "head"),
    )
    out_specs = (P("frame", "head"), P("frame", "head"))
    return jax.shard_map(shards, mesh=mesh, in_specs=in_specs, out_specs=out_specs, check_vma=False)
```

```python
import math

import jax
import jax.numpy as jnp
import numpy as np
from jax import lax
from jax.experimental import pallas as pl
from jax.experimental.pallas import tpu as pltpu
from jax.sharding import PartitionSpec as P

HD = 128
LEVELS = 4
flow_shift = 5.0
C = math.log2(math.e) / math.sqrt(HD)
F32 = jnp.float32
BF16 = jnp.bfloat16
NY, NXL, NZ = 4, 2, 8
SIBLING = [(0, 1), (1, 0), (2, 3), (3, 2)]
PARTNER = [(0, 2), (2, 0), (1, 3), (3, 1)]


def noise_level(point):
    return flow_shift * point / (1.0 + (flow_shift - 1.0) * point)


def ring(value, by):
    n = lax.axis_size("frame")
    return lax.ppermute(value, "frame", [(i, (i + by) % n) for i in range(n)])


def swap(value, pairs):
    return lax.ppermute(value, "head", pairs)


NT = (((1,), (1,)), ((), ()))
ON_CHIP = pl.BlockSpec(memory_space=pltpu.VMEM)
SCALARS = pl.BlockSpec(memory_space=pltpu.SMEM)
CHUNK = 256
META = 16


def attend_own(meta, q_ref, k, v, o_ref):
    rows, width = q_ref.shape
    for c in range(rows // CHUNK):
        cs = pl.ds(c * CHUNK, CHUNK)
        lane = lax.broadcasted_iota(jnp.int32, (CHUNK, HD), 1)
        side = jnp.zeros((CHUNK, HD), F32)
        for i in range(meta.shape[0]):
            side = jnp.where(lane == META + i, meta[i].astype(F32), side)
        for h in range(width // HD):
            hs = pl.ds(h * HD, HD)
            s = lax.dot_general(q_ref[cs, hs], k[:, hs], NT, preferred_element_type=F32)
            m = jnp.max(s, axis=1, keepdims=True)
            p = jnp.exp2((s - m) * C)
            total = jnp.sum(p, axis=1, keepdims=True)
            o = jnp.dot(p.astype(BF16), v[:, hs], preferred_element_type=F32)
            o_ref[cs, hs] = (o * (1.0 / total)).astype(BF16)
            rest = m * C + jnp.log2(total)
            for i in range(3):
                part = rest.astype(BF16).astype(F32)
                side = jnp.where(lane == 3 * h + i, part, side)
                rest = rest - part
        o_ref[cs, pl.ds(width, HD)] = side.astype(BF16)


def attend_first(allow, q_ref, own, k1, v1, k2, v2, k3, acc_ref, p_ref):
    rows, width = k1.shape
    on = [jnp.where(allow[i] == 1, 1.0, 0.0) for i in range(4)]
    lane = lax.broadcasted_iota(jnp.int32, (CHUNK, HD), 1)
    for h in range(width // HD):
        hs = pl.ds(h * HD, HD)
        for c in range(rows // CHUNK):
            cs = pl.ds(c * CHUNK, CHUNK)
            q = q_ref[cs, hs]
            side = own[cs, pl.ds(width, HD)].astype(F32)
            top = jnp.sum(jnp.where(lane // 3 == h, side, 0.0), axis=1, keepdims=True)
            s = [lax.dot_general(q, k[:, hs], NT, preferred_element_type=F32) for k in (k1, k2, k3)]
            m = top
            for i in range(3):
                m = jnp.where(allow[i + 1] == 1, jnp.maximum(m, jnp.max(s[i], axis=1, keepdims=True) * C), m)
            p = [jnp.exp2((s[i] * C - m) * on[i + 1]) for i in range(3)]
            first = jnp.exp2(top - m)
            total = first
            for i in range(3):
                total += on[i + 1] * jnp.sum(p[i], axis=1, keepdims=True)
            inverse = 1.0 / total
            acc = first * own[cs, hs].astype(F32)
            for i, v in ((0, v1), (1, v2)):
                acc += on[i + 1] * jnp.dot(p[i].astype(BF16), v[:, hs], preferred_element_type=F32)
            acc_ref[cs, hs] = acc * inverse
            p_ref[h, cs, :] = (p[2] * (inverse * on[3])).astype(BF16)


def attend_last(acc_ref, p_ref, v3, o_ref):
    for h in range(v3.shape[1] // HD):
        hs = pl.ds(h * HD, HD)
        o_ref[:, hs] = (acc_ref[:, hs] + jnp.dot(p_ref[h], v3[:, hs], preferred_element_type=F32)).astype(BF16)


def kernel_call(body, ints, args, outs, name, flops, exps=0, space=44):
    moved = sum(a.size * a.dtype.itemsize for a in (*args, *outs))
    return pl.pallas_call(
        body,
        in_specs=[SCALARS] * len(ints) + [ON_CHIP] * len(args),
        out_specs=[ON_CHIP] * len(outs),
        out_shape=outs,
        compiler_params=pltpu.CompilerParams(vmem_limit_bytes=space * 2**20),
        cost_estimate=pl.CostEstimate(flops=1, transcendentals=0, bytes_accessed=1),
        name=name,
    )(*ints, *args)


def project_near(a0, a1, w0, w1, t):
    t[...] = jnp.dot(a0[...], w0[...], preferred_element_type=F32)
    t[...] += jnp.dot(a1[...], w1[...], preferred_element_type=F32)


def project_far(ints, t, a2, a3, w2, w3, gate, columns):
    k = a2.shape[1]
    swapped = ints[1] == 1
    x2 = jnp.where(swapped, a3[...], a2[...])
    x3 = jnp.where(swapped, a2[...], a3[...])
    total = t[:, columns] + jnp.dot(x2, w2[:, columns], preferred_element_type=F32)
    total += jnp.dot(x3, w3[:, columns], preferred_element_type=F32)
    return gate[pl.ds(ints[0], 1), columns] * total


def project_velocity(ints, t, a2, a3, w2, w3, gate, out):
    for j in range(out.shape[1] // CHUNK):
        columns = pl.ds(j * CHUNK, CHUNK)
        out[:, columns] = project_far(ints, t, a2, a3, w2, w3, gate, columns).astype(BF16)


def project_next(ints, delta, t, a2, a3, w2, w3, gate, lat_a, lat_b, fresh, out):
    half = lat_a.shape[0]
    for j in range(out.shape[1] // CHUNK):
        columns = pl.ds(j * CHUNK, CHUNK)
        update = delta[0] * project_far(ints, t, a2, a3, w2, w3, gate, columns)
        for i, lat in enumerate((lat_a, lat_b)):
            rows = pl.ds(i * half, half)
            new = (lat[:, columns].astype(F32) + update[i * half : (i + 1) * half]).astype(BF16)
            out[rows, columns] = jnp.where(ints[2] == 1, fresh[rows, columns], new)


def both(pairs_of):
    pairs = []
    for place in np.ndindex(NY, NXL, NZ, 2, 2):
        (y, x_lo, z, x_hi, core), (y2, x_lo2, z2, x_hi2, core2) = place, pairs_of(*place)
        number = lambda y, x_lo, z, x_hi, core: ((y * NXL + x_lo) * NZ + z) * 4 + x_hi * 2 + core
        pairs.append((number(*place), number(y2, x_lo2, z2, x_hi2, core2)))
    return pairs


def across(value):
    pairs = both(lambda y, x_lo, z, x_hi, core: (y, 1 - x_lo, z, 1 - x_hi, core ^ (y % 2)))
    return lax.ppermute(value, ("frame", "head"), pairs)


def shards(latents, queries, keys, values, out_weight, gate_table, levels, block_mask, fresh):
    frame = lax.axis_index("frame")
    head = lax.axis_index("head")
    spans = lax.axis_size("frame")
    window = block_mask.shape[1]
    rows, width = latents.shape
    rows_w = out_weight.shape[0]
    heads = queries.shape[1] // HD
    barrier = lax.optimization_barrier

    odd = (frame // (NXL * NZ)) % 2
    core = head % 2
    other = (1 - head // 2) * 2 + (core ^ odd)
    columns_of = lambda weight, at: lax.dynamic_slice(weight, (0, at * width), (rows_w, width))

    work = heads * rows * rows
    k_r1 = ring(keys, 1)
    v_r1 = ring(values, 1)
    q_next = ring(queries, -1)
    lat_a = ring(latents[: rows // 2], -1)
    w_far = across(columns_of(out_weight, other))
    (own,) = kernel_call(
        attend_own,
        (jnp.concatenate([block_mask[0], levels]),),
        (queries, keys, values),
        (jax.ShapeDtypeStruct((rows, heads * HD + HD), BF16),),
        "attend_own",
        4 * work * HD,
        work,
    )
    k_r1, v_r1, q_next, lat_a, own, w_own, w_sib = barrier(
        (k_r1, v_r1, q_next, lat_a, own, columns_of(out_weight, head), columns_of(out_weight, head ^ 1))
    )

    k_r2 = ring(k_r1, 1)
    v_r2 = ring(v_r1, 1)
    own = ring(own, -1)
    own, w_far, lat_b = barrier((own, w_far, latents[rows // 2 :]))
    lat_b = ring(lat_b, -1)
    w_far2 = lax.ppermute(
        w_far, "frame", [(i, (((i // 16) ^ 1) * 16) + i % 16) for i in range(NY * NXL * NZ)]
    )
    at = heads * HD + META
    meta_next = own[0, at : at + window + 1].astype(jnp.int32)

    span = lax.rem(frame + 1, spans)
    distances = jnp.arange(window, dtype=jnp.int32)
    allow = ((meta_next[:window] == 1) & (span - distances >= 0)).astype(jnp.int32)
    half = jax.ShapeDtypeStruct((rows, heads * HD), F32)
    acc, p3 = kernel_call(
        attend_first,
        (allow,),
        (q_next, own, keys, values, k_r1, v_r1, k_r2),
        (half, jax.ShapeDtypeStruct((heads, rows, rows), BF16)),
        "attend_first",
        10 * work * HD,
        3 * work,
    )
    v_r2, lat_b = barrier((v_r2, lat_b))
    (attended,) = kernel_call(
        attend_last,
        (),
        (acc, p3, v_r2),
        (jax.ShapeDtypeStruct((rows, heads * HD), BF16),),
        "attend_last",
        2 * work * HD,
    )

    attended, w_own, w_sib = barrier((attended, w_own, w_sib))
    mine = ring(attended, 1)
    partner1 = swap(attended, PARTNER)
    sibling1 = swap(attended, SIBLING)
    w_sib = swap(w_sib, SIBLING)
    near = jax.ShapeDtypeStruct((rows, width), F32)
    flops = 4 * rows * width * heads * HD
    (t1,) = kernel_call(project_near, (), (attended, sibling1, w_own, w_sib), (near,), "near_next", flops, space=24)
    def scalars(level):
        at = level.astype(F32)
        delta = noise_level(at / LEVELS) - noise_level((at + 1.0) / LEVELS)
        is_last = (frame == spans - 1).astype(jnp.int32)
        return jnp.stack([level, odd, is_last]), delta[None]

    ints1, delta = scalars(meta_next[window])
    ints2, _ = scalars(levels[0])
    partner1, mine, t1, ints1, delta, ints2 = barrier((partner1, mine, t1, ints1, delta, ints2))
    partner2 = swap(mine, PARTNER)
    sibling2 = swap(mine, SIBLING)
    (t2,) = kernel_call(
        project_near, (), (mine, sibling2, w_own, w_sib), (near,), "near_velocity", flops, space=24
    )
    other1 = swap(partner1, SIBLING)
    out = jax.ShapeDtypeStruct((rows, width), BF16)
    (next_latents,) = kernel_call(
        project_next,
        (ints1, delta),
        (t1, partner1, other1, w_far, w_far2, gate_table, lat_a, lat_b, fresh),
        (out,),
        "project_next",
        flops,
        space=24,
    )
    partner2, t2 = barrier((partner2, t2))
    other2 = swap(partner2, SIBLING)
    (velocity,) = kernel_call(
        project_velocity,
        (ints2,),
        (t2, partner2, other2, w_far, w_far2, gate_table),
        (out,),
        "project_velocity",
        flops,
        space=24,
    )
    return velocity, next_latents


def solution(mesh):
    in_specs = (
        P("frame", "head"),
        P("frame", "head"),
        P("frame", "head"),
        P("frame", "head"),
        P("head", None),
        P(None, "head"),
        P("frame"),
        P("frame", None),
        P(None, "head"),
    )
    out_specs = (P("frame", "head"), P("frame", "head"))
    return jax.shard_map(shards, mesh=mesh, in_specs=in_specs, out_specs=out_specs, check_vma=False)
```

```python
import math

import jax
import jax.numpy as jnp
import numpy as np
from jax import lax
from jax.experimental import pallas as pl
from jax.experimental.pallas import tpu as pltpu
from jax.sharding import PartitionSpec as P

HD = 128
LEVELS = 4
flow_shift = 5.0
C = math.log2(math.e) / math.sqrt(HD)
F32 = jnp.float32
BF16 = jnp.bfloat16
NY, NXL, NZ = 4, 2, 8
SIBLING = [(0, 1), (1, 0), (2, 3), (3, 2)]
PARTNER = [(0, 2), (2, 0), (1, 3), (3, 1)]


def noise_level(point):
    return flow_shift * point / (1.0 + (flow_shift - 1.0) * point)


def ring(value, by):
    n = lax.axis_size("frame")
    return lax.ppermute(value, "frame", [(i, (i + by) % n) for i in range(n)])


def swap(value, pairs):
    return lax.ppermute(value, "head", pairs)


NT = (((1,), (1,)), ((), ()))
ON_CHIP = pl.BlockSpec(memory_space=pltpu.VMEM)
SCALARS = pl.BlockSpec(memory_space=pltpu.SMEM)
CHUNK = 256
META = 16


def attend_own(meta, q_ref, k, v, o_ref):
    rows, width = q_ref.shape
    for c in range(rows // CHUNK):
        cs = pl.ds(c * CHUNK, CHUNK)
        lane = lax.broadcasted_iota(jnp.int32, (CHUNK, HD), 1)
        side = jnp.zeros((CHUNK, HD), F32)
        for i in range(meta.shape[0]):
            side = jnp.where(lane == META + i, meta[i].astype(F32), side)
        for h in range(width // HD):
            hs = pl.ds(h * HD, HD)
            s = lax.dot_general(q_ref[cs, hs], k[:, hs], NT, preferred_element_type=F32)
            m = jnp.max(s, axis=1, keepdims=True)
            p = jnp.exp2((s - m) * C)
            total = jnp.sum(p, axis=1, keepdims=True)
            o = jnp.dot(p.astype(BF16), v[:, hs], preferred_element_type=F32)
            o_ref[cs, hs] = (o * (1.0 / total)).astype(BF16)
            rest = m * C + jnp.log2(total)
            for i in range(3):
                part = rest.astype(BF16).astype(F32)
                side = jnp.where(lane == 3 * h + i, part, side)
                rest = rest - part
        o_ref[cs, pl.ds(width, HD)] = side.astype(BF16)


def attend_first(allow, q_ref, own, k1, v1, k2, v2, k3, acc_ref, p_ref):
    rows, width = k1.shape
    on = [jnp.where(allow[i] == 1, 1.0, 0.0) for i in range(4)]
    lane = lax.broadcasted_iota(jnp.int32, (CHUNK, HD), 1)
    for h in range(width // HD):
        hs = pl.ds(h * HD, HD)
        for c in range(rows // CHUNK):
            cs = pl.ds(c * CHUNK, CHUNK)
            q = q_ref[cs, hs]
            side = own[cs, pl.ds(width, HD)].astype(F32)
            top = jnp.sum(jnp.where(lane // 3 == h, side, 0.0), axis=1, keepdims=True)
            s = [lax.dot_general(q, k[:, hs], NT, preferred_element_type=F32) for k in (k1, k2, k3)]
            m = top
            for i in range(3):
                m = jnp.where(allow[i + 1] == 1, jnp.maximum(m, jnp.max(s[i], axis=1, keepdims=True) * C), m)
            p = [jnp.exp2((s[i] * C - m) * on[i + 1]) for i in range(3)]
            first = jnp.exp2(top - m)
            total = first
            for i in range(3):
                total += on[i + 1] * jnp.sum(p[i], axis=1, keepdims=True)
            inverse = 1.0 / total
            acc = first * own[cs, hs].astype(F32)
            for i, v in ((0, v1), (1, v2)):
                acc += on[i + 1] * jnp.dot(p[i].astype(BF16), v[:, hs], preferred_element_type=F32)
            acc_ref[cs, hs] = acc * inverse
            p_ref[h, cs, :] = (p[2] * (inverse * on[3])).astype(BF16)


def attend_last(acc_ref, p_ref, v3, o_ref):
    for h in range(v3.shape[1] // HD):
        hs = pl.ds(h * HD, HD)
        o_ref[:, hs] = (acc_ref[:, hs] + jnp.dot(p_ref[h], v3[:, hs], preferred_element_type=F32)).astype(BF16)


def kernel_call(body, ints, args, outs, name, flops, exps=0, space=44):
    moved = sum(a.size * a.dtype.itemsize for a in (*args, *outs))
    return pl.pallas_call(
        body,
        in_specs=[SCALARS] * len(ints) + [ON_CHIP] * len(args),
        out_specs=[ON_CHIP] * len(outs),
        out_shape=outs,
        compiler_params=pltpu.CompilerParams(vmem_limit_bytes=space * 2**20),
        cost_estimate=pl.CostEstimate(flops=1, transcendentals=0, bytes_accessed=1),
        name=name,
    )(*ints, *args)


def project_near(a0, a1, w0, w1, t):
    t[...] = jnp.dot(a0[...], w0[...], preferred_element_type=F32)
    t[...] += jnp.dot(a1[...], w1[...], preferred_element_type=F32)


def in_order(ints, a2, a3):
    swapped = ints[1] == 1
    return jnp.where(swapped, a3[...], a2[...]), jnp.where(swapped, a2[...], a3[...])


def project_far(ints, t, x2, x3, w2, w3, gate, columns):
    total = t[:, columns] + jnp.dot(x2, w2[:, columns], preferred_element_type=F32)
    total += jnp.dot(x3, w3[:, columns], preferred_element_type=F32)
    return gate[pl.ds(ints[0], 1), columns] * total


def project_velocity(ints, t, a2, a3, w2, w3, gate, out):
    x2, x3 = in_order(ints, a2, a3)
    for j in range(out.shape[1] // CHUNK):
        columns = pl.ds(j * CHUNK, CHUNK)
        out[:, columns] = project_far(ints, t, x2, x3, w2, w3, gate, columns).astype(BF16)


def project_next(ints, delta, t, a2, a3, w2, w3, gate, lat_a, lat_b, fresh, out):
    x2, x3 = in_order(ints, a2, a3)
    half = lat_a.shape[0]
    for j in range(out.shape[1] // CHUNK):
        columns = pl.ds(j * CHUNK, CHUNK)
        update = delta[0] * project_far(ints, t, x2, x3, w2, w3, gate, columns)
        for i, lat in enumerate((lat_a, lat_b)):
            rows = pl.ds(i * half, half)
            new = (lat[:, columns].astype(F32) + update[i * half : (i + 1) * half]).astype(BF16)
            out[rows, columns] = jnp.where(ints[2] == 1, fresh[rows, columns], new)


def both(pairs_of):
    pairs = []
    for place in np.ndindex(NY, NXL, NZ, 2, 2):
        (y, x_lo, z, x_hi, core), (y2, x_lo2, z2, x_hi2, core2) = place, pairs_of(*place)
        number = lambda y, x_lo, z, x_hi, core: ((y * NXL + x_lo) * NZ + z) * 4 + x_hi * 2 + core
        pairs.append((number(*place), number(y2, x_lo2, z2, x_hi2, core2)))
    return pairs


def across(value):
    pairs = both(lambda y, x_lo, z, x_hi, core: (y, 1 - x_lo, z, 1 - x_hi, core ^ (y % 2)))
    return lax.ppermute(value, ("frame", "head"), pairs)


def shards(latents, queries, keys, values, out_weight, gate_table, levels, block_mask, fresh):
    frame = lax.axis_index("frame")
    head = lax.axis_index("head")
    spans = lax.axis_size("frame")
    window = block_mask.shape[1]
    rows, width = latents.shape
    rows_w = out_weight.shape[0]
    heads = queries.shape[1] // HD
    barrier = lax.optimization_barrier

    odd = (frame // (NXL * NZ)) % 2
    core = head % 2
    other = (1 - head // 2) * 2 + (core ^ odd)
    columns_of = lambda weight, at: lax.dynamic_slice(weight, (0, at * width), (rows_w, width))

    work = heads * rows * rows
    k_r1 = ring(keys, 1)
    v_r1 = ring(values, 1)
    q_next = ring(queries, -1)
    lat_a = ring(latents[: rows // 2], -1)
    w_far = across(columns_of(out_weight, other))
    (own,) = kernel_call(
        attend_own,
        (jnp.concatenate([block_mask[0], levels]),),
        (queries, keys, values),
        (jax.ShapeDtypeStruct((rows, heads * HD + HD), BF16),),
        "attend_own",
        4 * work * HD,
        work,
    )
    k_r1, v_r1, q_next, lat_a, own, w_own, w_sib = barrier(
        (k_r1, v_r1, q_next, lat_a, own, columns_of(out_weight, head), columns_of(out_weight, head ^ 1))
    )

    k_r2 = ring(k_r1, 1)
    v_r2 = ring(v_r1, 1)
    own = ring(own, -1)
    own, w_far, lat_b = barrier((own, w_far, latents[rows // 2 :]))
    lat_b = ring(lat_b, -1)
    w_far2 = lax.ppermute(
        w_far, "frame", [(i, (((i // 16) ^ 1) * 16) + i % 16) for i in range(NY * NXL * NZ)]
    )
    at = heads * HD + META
    meta_next = own[0, at : at + window + 1].astype(jnp.int32)

    span = lax.rem(frame + 1, spans)
    distances = jnp.arange(window, dtype=jnp.int32)
    allow = ((meta_next[:window] == 1) & (span - distances >= 0)).astype(jnp.int32)
    half = jax.ShapeDtypeStruct((rows, heads * HD), F32)
    acc, p3 = kernel_call(
        attend_first,
        (allow,),
        (q_next, own, keys, values, k_r1, v_r1, k_r2),
        (half, jax.ShapeDtypeStruct((heads, rows, rows), BF16)),
        "attend_first",
        10 * work * HD,
        3 * work,
    )
    v_r2, lat_b = barrier((v_r2, lat_b))
    (attended,) = kernel_call(
        attend_last,
        (),
        (acc, p3, v_r2),
        (jax.ShapeDtypeStruct((rows, heads * HD), BF16),),
        "attend_last",
        2 * work * HD,
    )

    attended, w_own, w_sib = barrier((attended, w_own, w_sib))
    mine = ring(attended, 1)
    partner1 = swap(attended, PARTNER)
    sibling1 = swap(attended, SIBLING)
    w_sib = swap(w_sib, SIBLING)
    near = jax.ShapeDtypeStruct((rows, width), F32)
    flops = 4 * rows * width * heads * HD
    (t1,) = kernel_call(project_near, (), (attended, sibling1, w_own, w_sib), (near,), "near_next", flops, space=24)
    def scalars(level):
        at = level.astype(F32)
        delta = noise_level(at / LEVELS) - noise_level((at + 1.0) / LEVELS)
        is_last = (frame == spans - 1).astype(jnp.int32)
        return jnp.stack([level, odd, is_last]), delta[None]

    ints1, delta = scalars(meta_next[window])
    ints2, _ = scalars(levels[0])
    partner1, mine, t1, ints1, delta, ints2 = barrier((partner1, mine, t1, ints1, delta, ints2))
    partner2 = swap(mine, PARTNER)
    sibling2 = swap(mine, SIBLING)
    (t2,) = kernel_call(
        project_near, (), (mine, sibling2, w_own, w_sib), (near,), "near_velocity", flops, space=24
    )
    other1 = swap(partner1, SIBLING)
    out = jax.ShapeDtypeStruct((rows, width), BF16)
    (next_latents,) = kernel_call(
        project_next,
        (ints1, delta),
        (t1, partner1, other1, w_far, w_far2, gate_table, lat_a, lat_b, fresh),
        (out,),
        "project_next",
        flops,
        space=24,
    )
    partner2, t2 = barrier((partner2, t2))
    other2 = swap(partner2, SIBLING)
    (velocity,) = kernel_call(
        project_velocity,
        (ints2,),
        (t2, partner2, other2, w_far, w_far2, gate_table),
        (out,),
        "project_velocity",
        flops,
        space=24,
    )
    return velocity, next_latents


def solution(mesh):
    in_specs = (
        P("frame", "head"),
        P("frame", "head"),
        P("frame", "head"),
        P("frame", "head"),
        P("head", None),
        P(None, "head"),
        P("frame"),
        P("frame", None),
        P(None, "head"),
    )
    out_specs = (P("frame", "head"), P("frame", "head"))
    return jax.shard_map(shards, mesh=mesh, in_specs=in_specs, out_specs=out_specs, check_vma=False)
```
